32 devices in a mesh: seq: 4 (over z), head: 4 (over y, x), dp: 2 (over core).
Axes of the slice: x: 2, y: 2, z: 4, core: 2. Of those that a mesh axis runs over, the one named last changes fastest.
Arguments:
- inputs: bfloat16 [4096, 4096], P(('dp', 'seq'), 'head'), parts along dimension 0, may hold values from -2 to 2
- step_raw: float32 [4096, 64], P(('dp', 'seq'), 'head'), parts along dimension 0, may hold values from -5 to 600
- decay_rate: float32 [64], P('head'), may hold values from 0.002 to 0.1
- skip_gain: float32 [64], P('head'), may hold values from 0.3 to 3
- b_proj: bfloat16 [4096, 8, 256], P(('dp', 'seq')), parts along dimension 0, may hold values from -2 to 2
- c_proj: bfloat16 [4096, 8, 256], P(('dp', 'seq')), parts along dimension 0, may hold values from -2 to 2
- lengths: int32 [4], P('dp'), parts along dimension 0, may hold values from 1 to 512, as said below
- cotangent: bfloat16 [4096, 4096], P(('dp', 'seq'), 'head'), parts along dimension 0, may hold values from -1.5 to 1.5
Outputs:
- outputs: bfloat16 [4096, 4096], P(('dp', 'seq'), 'head'), parts along dimension 0
- grad_inputs: bfloat16 [4096, 4096], P(('dp', 'seq'), 'head'), parts along dimension 0
- grad_step: float32 [4096, 64], P(('dp', 'seq'), 'head'), parts along dimension 0
- grad_b: float32 [4096, 8, 256], P(('dp', 'seq', 'head')), parts along dimension 0
- grad_c: float32 [4096, 8, 256], P(('dp', 'seq', 'head')), parts along dimension 0
The draws below stay inside these ranges and needn't reach their ends.
There are 2 independent parts, one for each index of `dp`. The reference program is written for one: setup_inputs(seed, part) draws one part's arguments, and reference() takes and returns one part's arrays. A program takes and returns all parts, laid end to end along the dimension named above; an argument that names none is the same for every part. Nothing has to cross between parts.
Inputs may be any that keep to these rules, and one draw needn't show every extreme that they name: `lengths`: some response has exactly 512 tokens.
All inputs are finite; a program needn't handle non-finite values.
Results may differ from the reference program's by a relative error of at most 0.009.
Values sent between devices are 32-bit elements; how exact they have to be, the bound alone decides.
A program may use at most 128 MiB of HBM per device.

```python
import math
import jax
import jax.numpy as jnp
from jax import lax

HEADDIM = 64
DSTATE = 256
GROUPS = 8
NHEADS = 64
BLOCK = 256
SLOT_LEN = 512
SEQS_DEV = 1
PREFIX_DEVS = 2
TOKENS = 2048
RESPONSES = 2
N_SEQ = 4
N_HEAD = 4


def marked_entries(key):
    marked_key, level_key = jax.random.split(jax.random.fold_in(key, 11), 2)
    shape_extents = (TOKENS, NHEADS)
    marked = jax.random.uniform(marked_key, shape_extents, jnp.float32) < 0.0025
    level = jax.random.uniform(level_key, shape_extents, jnp.float32, 200.0, 600.0)
    return (marked, level)


def draw_step_raw(key, part):
    value_key = jax.random.fold_in(key, 13)
    shape_extents = (TOKENS, NHEADS)
    value_rows = jnp.clip(jax.random.normal(value_key, shape_extents, jnp.float32) * 0.8 - 1.0, -5.0, 3.0)
    marked, level = marked_entries(key)
    return jnp.where(marked, level, value_rows).astype(jnp.float32)


def draw_inputs(key, part):
    noise_key = jax.random.fold_in(key, 17)
    shape_extents = (TOKENS, NHEADS * HEADDIM)
    base_rows = jnp.clip(jax.random.normal(noise_key, shape_extents, jnp.float32) * 0.5, -2.0, 2.0)
    marked, level = marked_entries(key)
    factor = jnp.where(marked, 1.0 / level, 1.0)
    factor_wide = jnp.repeat(factor, HEADDIM, axis=1)
    return (base_rows * factor_wide).astype(jnp.bfloat16)


def draw_lengths(key, part):
    key_vals, key_spot = jax.random.split(jax.random.fold_in(key, 23), 2)
    values = jax.random.randint(key_vals, (RESPONSES,), 1, SLOT_LEN + 1, dtype=jnp.int32)
    long_spot = jax.random.randint(key_spot, (), 0, RESPONSES, dtype=jnp.int32)
    return values.at[long_spot].set(SLOT_LEN).astype(jnp.int32)


def block_scale(key, shape, cuts, least, high):
    def one(position, parts):
        steps = jax.random.uniform(jax.random.fold_in(jax.random.fold_in(key, 6), position), (parts,), jnp.float32, least / len(cuts), high / len(cuts))
        return jnp.repeat(jnp.exp(steps), shape[position] // parts).reshape((-1,) + (1,) * (len(shape) - position - 1))

    level = one(*cuts[0])
    for cut in cuts[1:]:
        level = level * one(*cut)
    return level


def normal_values(rng, extent, scale, reach, cuts=(), held_as=jnp.bfloat16):
    entries = scale * jax.random.normal(rng, extent, jnp.float32)
    if cuts:
        entries = entries * block_scale(rng, extent, cuts, -0.22, 0.18)
    return jnp.clip(entries, -reach, reach).astype(held_as)


def setup_inputs(seed: int = 0, part: int = 0) -> dict:
    keys = jax.random.split(jax.random.key(seed), 9)
    part_keys = jax.random.split(jax.random.fold_in(keys[8], part), 9)
    return {
        "inputs": draw_inputs(jax.random.fold_in(jax.random.fold_in(keys[8], part), 71), part),
        "step_raw": draw_step_raw(jax.random.fold_in(jax.random.fold_in(keys[8], part), 71), part),
        "decay_rate": jnp.clip(jnp.exp(math.log(0.1) - 3.912023 * jax.random.uniform(keys[2], (NHEADS,), jnp.float32) ** block_scale(keys[2], (NHEADS,), ((0, 4),), -0.2, 0.2)), 0.002, 0.1),
        "skip_gain": jnp.clip(jnp.exp(math.log(3.0) - 2.3025851 * jax.random.uniform(keys[3], (NHEADS,), jnp.float32) ** block_scale(keys[3], (NHEADS,), ((0, 4),), -0.2, 0.2)), 0.3, 3.0),
        "b_proj": normal_values(part_keys[4], (TOKENS, GROUPS, DSTATE), 0.3, 2.0, ((0, 4),)),
        "c_proj": normal_values(part_keys[5], (TOKENS, GROUPS, DSTATE), 0.3, 2.0, ((0, 4),)),
        "lengths": draw_lengths(jax.random.fold_in(jax.random.fold_in(keys[8], part), 71), part),
        "cotangent": normal_values(part_keys[7], (TOKENS, NHEADS * HEADDIM), 0.2, 1.5, ((0, 4), (1, 4))),
    }


PRECISE = lax.Precision.HIGHEST

def step_sizes(step_rows, decay_rate, mask_rows, seq_count, block_len, groups):
    step_size = jax.nn.softplus(step_rows) * mask_rows[:, None]
    head_count = decay_rate.shape[0]
    five_dims = (seq_count, -1, block_len, head_count // groups, groups)
    return (step_size.reshape(five_dims), (-(step_size * decay_rate[None, :])).reshape(five_dims))

def main_terms(in_rows, step_rows, b_rows, c_rows, decay_rate, skip_gain, mask_rows, seq_count, block_len):
    groups, state_dim = (b_rows.shape[1], b_rows.shape[2])
    head_count = decay_rate.shape[0]
    head_width = in_rows.shape[1] // head_count
    per_group = head_count // groups
    step_size, log_step = step_sizes(step_rows, decay_rate, mask_rows, seq_count, block_len, groups)
    within = jnp.cumsum(log_step, axis=2)
    totals = within[:, :, -1]
    blocks = within.shape[1]
    x_dims = (seq_count, blocks, block_len, per_group, groups, head_width)
    g_dims = (seq_count, blocks, block_len, groups, state_dim)
    x_round = in_rows.astype(jnp.bfloat16).astype(jnp.float32).reshape(x_dims)
    b_round = b_rows.astype(jnp.bfloat16).astype(jnp.float32).reshape(g_dims)
    c_round = c_rows.astype(jnp.bfloat16).astype(jnp.float32).reshape(g_dims)
    scores = jnp.einsum('sktgn,skugn->skgtu', c_round, b_round, precision=PRECISE)
    within_t = jnp.moveaxis(within, 2, -1)
    spread = within_t[..., :, None] - within_t[..., None, :]
    causal = jnp.arange(block_len)[:, None] >= jnp.arange(block_len)[None, :]
    decays = jnp.where(causal, jnp.exp(jnp.where(causal, spread, 0.0)), 0.0)
    weights = (scores[:, :, None] * decays * jnp.moveaxis(step_size, 2, -1)[..., None, :]).astype(jnp.bfloat16)
    inside = jnp.einsum('skmgtu,skumgp->sktmgp', weights.astype(jnp.float32), x_round, precision=PRECISE)
    scaled = (in_rows.reshape(x_dims) * (step_size * jnp.exp(totals[:, :, None] - within))[..., None]).astype(jnp.bfloat16)
    block_states = jnp.einsum('skugn,skumgp->skmgnp', b_round, scaled.astype(jnp.float32), precision=PRECISE)
    running = jnp.zeros((seq_count, per_group, groups, state_dim, head_width), jnp.float32)
    entering = []
    for block_index in range(blocks):
        entering.append(running)
        running = jnp.exp(totals[:, block_index])[..., None, None] * running + block_states[:, block_index]
    entered = jnp.stack(entering, axis=1)
    across = jnp.einsum('sktgn,skmgnp->sktmgp', c_rows.reshape(g_dims), entered, precision=PRECISE) * jnp.exp(within)[..., None]
    skip_term = skip_gain.reshape(per_group, groups)[:, :, None] * in_rows.reshape(x_dims)
    result = (inside + across + skip_term) * mask_rows.reshape(seq_count, blocks, block_len, 1, 1, 1)
    return (result.reshape(in_rows.shape), lax.optimization_barrier(jnp.sum(totals, axis=1)), running)

def corr_terms(step_rows, c_rows, start_rows, decay_rate, mask_rows, seq_count, block_len):
    groups, state_dim = (c_rows.shape[1], c_rows.shape[2])
    head_count = decay_rate.shape[0]
    step_size, log_step = step_sizes(step_rows, decay_rate, mask_rows, seq_count, block_len, groups)
    blocks = log_step.shape[1]
    whole = jnp.cumsum(log_step.reshape(seq_count, blocks * block_len, head_count // groups, groups), axis=1).reshape(log_step.shape)
    c_dims = (seq_count, blocks, block_len, groups, state_dim)
    result = jnp.einsum('sktgn,smgnp->sktmgp', c_rows.reshape(c_dims), start_rows, precision=PRECISE) * jnp.exp(whole)[..., None]
    result = result * mask_rows.reshape(seq_count, blocks, block_len, 1, 1, 1)
    return result.reshape(c_rows.shape[0], -1)

def reference(inputs, step_raw, decay_rate, skip_gain, b_proj, c_proj, lengths, cotangent):
    row_count = SEQS_DEV * SLOT_LEN
    slot_ids = jnp.arange(SLOT_LEN, dtype=jnp.int32)
    resp_mask = (slot_ids[None, :] < lengths[:, None]).astype(jnp.float32).reshape(-1)
    full_mask = jnp.concatenate([jnp.ones((PREFIX_DEVS * row_count,), jnp.float32), resp_mask]).reshape(N_SEQ, row_count)
    b_full = b_proj.astype(jnp.float32)
    c_full = c_proj.astype(jnp.float32)

    def per_device(array):
        return array.reshape((N_SEQ, row_count) + array.shape[1:])

    def shard_forward(in_rows, step_rows, b_rows, c_rows, rate_rows, gain_rows):

        def local_part(in_dev, step_dev, b_dev, c_dev, mask_dev):
            return main_terms(in_dev, step_dev, b_dev, c_dev, rate_rows, gain_rows, mask_dev, SEQS_DEV, BLOCK)
        local_out, log_total, local_state = jax.vmap(local_part)(per_device(in_rows), per_device(step_rows), per_device(b_rows), per_device(c_rows), full_mask)
        running = jnp.zeros(local_state.shape[1:], jnp.float32)
        starts = []
        for piece in range(PREFIX_DEVS):
            starts.append(running)
            running = jnp.exp(log_total[piece])[..., None, None] * running + local_state[piece]
        responded = jnp.broadcast_to(running[None], (N_SEQ - PREFIX_DEVS,) + running.shape)
        start_all = jnp.concatenate([jnp.stack(starts), responded])

        def corr_part(step_dev, c_dev, start_dev, mask_dev):
            return corr_terms(step_dev, c_dev, start_dev, rate_rows, mask_dev, SEQS_DEV, BLOCK)
        correction = jax.vmap(corr_part)(per_device(step_rows), per_device(c_rows), start_all, full_mask)
        return (local_out + correction).reshape(TOKENS, -1)

    def per_shard(totals_carry, pieces):
        in_piece, step_piece, cot_piece, rate_piece, gain_piece = pieces

        def forward(in_rows, step_rows, b_rows, c_rows):
            return shard_forward(in_rows, step_rows, b_rows, c_rows, rate_piece, gain_piece)
        y_full, backward = jax.vjp(forward, in_piece.astype(jnp.float32), step_piece, b_full, c_full)
        grad_x, grad_s, grad_bp, grad_cp = backward(cot_piece.astype(jnp.float32))
        return ((totals_carry[0] + grad_bp, totals_carry[1] + grad_cp), (y_full.astype(jnp.bfloat16), grad_x.astype(jnp.bfloat16), grad_s))

    def split_heads(array):
        return array.reshape(TOKENS, N_HEAD, -1).transpose(1, 0, 2)

    def join_heads(array):
        return array.transpose(1, 0, 2).reshape(TOKENS, -1)
    zero_grad = jnp.zeros(b_proj.shape, jnp.float32)
    (grad_b, grad_c), (outs_y, outs_x, outs_s) = lax.scan(per_shard, (zero_grad, zero_grad), (split_heads(inputs), split_heads(step_raw), split_heads(cotangent), decay_rate.reshape(N_HEAD, -1), skip_gain.reshape(N_HEAD, -1)))
    return (join_heads(outs_y), join_heads(outs_x), join_heads(outs_s), grad_b, grad_c)
```

```python
import functools

import jax
import jax.numpy as jnp
from jax import lax
from jax.experimental import pallas as pl
from jax.experimental.pallas import tpu as pltpu
from jax.sharding import PartitionSpec as P

BLOCK = 256
PREFIX_DEVS = 2
LANES = 128
F32 = jnp.float32
BF16 = jnp.bfloat16
EXACT = lax.Precision.HIGHEST


def mm(a, b, ca, cb):
    return lax.dot_general(a, b, (((ca,), (cb,)), ((), ())), preferred_element_type=F32)


def layer_kernel(
    peers, heads, groups,
    x_ref, dy_ref, b_ref, c_ref, small_ref, gain_ref, decay_ref,
    y_ref, dx_ref, gs_ref, db_ref, dc_ref,
    wi_b, dt_b, wi_t, dt_t, state, first_state, grad_own, later_grad,
    state_in, state_out, grad_in, grad_out, y_acc, dx_acc, q_acc, mask_b,
    fs_sem, fr_sem, bs_sem, br_sem,
):
    pos = lax.axis_index("seq")
    prefix = jnp.where(pos < PREFIX_DEVS, 1.0, 0.0).astype(F32)
    rows = x_ref.shape[0]
    blocks = rows // BLOCK
    pairs = groups // 2
    half = groups * 64
    low = lax.broadcasted_iota(jnp.int32, (1, LANES), 1) < 64

    barrier = pltpu.get_barrier_semaphore()

    @pl.when(pos > 0)
    def _():
        pl.semaphore_signal(barrier, inc=1, device_id={"seq": pos - 1}, device_id_type=pl.DeviceIdType.MESH)

    @pl.when(pos < peers - 1)
    def _():
        pl.semaphore_signal(barrier, inc=1, device_id={"seq": pos + 1}, device_id_type=pl.DeviceIdType.MESH)

    tri = lax.broadcasted_iota(jnp.int32, (BLOCK, BLOCK), 0) >= lax.broadcasted_iota(
        jnp.int32, (BLOCK, BLOCK), 1
    )

    def span(k):
        return slice(k * BLOCK, (k + 1) * BLOCK)

    for k in range(blocks):
        vals = small_ref[span(k), :]
        sums = lax.dot_general(
            tri.astype(F32), vals, (((1,), (0,)), ((), ())),
            preferred_element_type=F32, precision=EXACT,
        )
        wi_t[:, span(k)] = sums.T
        dt_t[:, span(k)] = vals.T
        for h in range(heads):
            wi_b[h, span(k), :] = jnp.broadcast_to(sums[:, heads + h : heads + h + 1], (BLOCK, LANES))
            dt_b[h, span(k), :] = jnp.broadcast_to(vals[:, h : h + 1], (BLOCK, LANES))
        mask_b[span(k), :] = jnp.broadcast_to(vals[:, 3 * heads : 3 * heads + 1], (BLOCK, LANES))

    def turn(v):
        return pltpu.roll(v, 64, 1)

    def slabs(ref, p):
        lo = ref[:, pl.ds(pl.multiple_of(p * LANES, LANES), LANES)].astype(F32)
        hi = ref[:, pl.ds(pl.multiple_of(half + p * LANES, LANES), LANES)].astype(F32)
        return lo, hi

    def join(lo, hi):
        return jnp.where(low, lo, turn(hi)), jnp.where(low, turn(lo), hi)

    def by_head(ref, g, k):
        return jnp.where(low, ref[g, span(k), :], ref[groups + g, span(k), :])

    def total(g, k):
        at = pl.ds((k + 1) * BLOCK - 1, 1)
        return jnp.where(low, wi_b[g, at, :], wi_b[groups + g, at, :])

    def hop_f(p):
        part = pl.ds(2 * p, 2)
        return pltpu.make_async_remote_copy(
            src_ref=state_out.at[part], dst_ref=state_in.at[part],
            send_sem=fs_sem.at[p], recv_sem=fr_sem.at[p],
            device_id={"seq": pos + 1}, device_id_type=pl.DeviceIdType.MESH,
        )

    def hop_b(p):
        part = pl.ds(2 * p, 2)
        return pltpu.make_async_remote_copy(
            src_ref=grad_out.at[part], dst_ref=grad_in.at[part],
            send_sem=bs_sem.at[p], recv_sem=br_sem.at[p],
            device_id={"seq": pos - 1}, device_id_type=pl.DeviceIdType.MESH,
        )

    def whole(g):
        return jnp.exp(prefix * (total(g, 0) + total(g, 1)))

    def pass_f(p):
        for j in range(2):
            g = 2 * p + j
            state_out[g] = whole(g) * state_in[g] + prefix * state[g]
        hop_f(p).start()

    def pass_b(p):
        for j in range(2):
            g = 2 * p + j
            grad_out[g] = whole(g) * grad_in[g] + grad_own[g]
        hop_b(p).start()

    @pl.when(pos == 0)
    def _():
        state_in[...] = jnp.zeros_like(state_in)

    @pl.when(pos == peers - 1)
    def _():
        grad_in[...] = jnp.zeros_like(grad_in)

    @pl.when(jnp.logical_or(pos == 0, pos == peers - 1))
    def _():
        pl.semaphore_wait(barrier, 1)

    @pl.when(jnp.logical_and(pos > 0, pos < peers - 1))
    def _():
        pl.semaphore_wait(barrier, 2)

    def local_states(p, carry):
        xs = join(*slabs(x_ref, p))
        dys = join(*slabs(dy_ref, p))
        for j in range(2):
            g = 2 * p + j
            adds, backs = [], []
            for k in range(blocks):
                wi = by_head(wi_b, g, k)
                dt = by_head(dt_b, g, k)
                scaled = (xs[j][span(k)] * (dt * jnp.exp(total(g, k) - wi))).astype(BF16)
                adds.append(mm(b_ref[g, span(k), :], scaled, 0, 0))
                lifted = (dys[j][span(k)] * mask_b[span(k), :] * jnp.exp(wi)).astype(BF16)
                backs.append(mm(c_ref[g, span(k), :], lifted, 0, 0))
            first_state[g] = adds[0]
            state[g] = jnp.exp(total(g, 1)) * adds[0] + adds[1]
            later_grad[g] = backs[1]
            grad_own[g] = backs[0] + jnp.exp(total(g, 0)) * backs[1]

        @pl.when(pos == 0)
        def _():
            pass_f(p)

        @pl.when(pos == peers - 1)
        def _():
            pass_b(p)

        return carry

    lax.fori_loop(0, pairs, local_states, 0)

    def inside(p, carry):
        xs = join(*slabs(x_ref, p))
        dys = join(*slabs(dy_ref, p))
        for j in range(2):
            g = 2 * p + j
            for k in range(blocks):
                b_blk = b_ref[g, span(k), :]
                c_blk = c_ref[g, span(k), :]
                scores = mm(c_blk, b_blk, 1, 1)
                x16 = xs[j][span(k)].astype(BF16)
                dyf = dys[j][span(k)] * mask_b[span(k), :]
                dy16 = dyf.astype(BF16)
                ys, dxs = [], []
                d_scores = None
                for m in range(2):
                    h = m * groups + g
                    col = wi_b[h, span(k), :]
                    col = jnp.concatenate([col, col], axis=1)
                    row = wi_t[pl.ds(heads + h, 1), span(k)]
                    decay = jnp.where(tri, jnp.exp(jnp.minimum(col - row, 0.0)), 0.0)
                    decay = decay * dt_t[pl.ds(h, 1), span(k)]
                    weights = (scores * decay).astype(BF16)
                    mine = low if m == 0 else jnp.logical_not(low)
                    dy_m = jnp.where(mine, dyf, 0.0).astype(BF16)
                    d_weights = mm(dy_m, x16, 1, 1) * decay
                    d_scores = d_weights if d_scores is None else d_scores + d_weights
                    ys.append(mm(weights, x16, 1, 0))
                    dxs.append(mm(weights, dy16, 0, 0))
                y_acc[g, span(k), :] = jnp.where(low, ys[0], ys[1])
                dx_acc[g, span(k), :] = jnp.where(low, dxs[0], dxs[1])
                ds16 = d_scores.astype(BF16)
                dc_ref[g, span(k), :] = mm(ds16, b_blk, 1, 0)
                db_ref[g, span(k), :] = mm(ds16, c_blk, 0, 0)

        @pl.when(jnp.logical_and(pos > 0, pos < peers - 1))
        def _():
            hop_f(p).wait_recv()
            pass_f(p)
            hop_b(p).wait_recv()
            pass_b(p)

        return carry

    lax.fori_loop(0, pairs, inside, 0)

    q_acc[...] = jnp.zeros_like(q_acc)
    last = lax.broadcasted_iota(jnp.int32, (BLOCK, 1), 0) == BLOCK - 1
    pick_row = lax.broadcasted_iota(jnp.int32, (4 * LANES, LANES), 0)
    pick_col = lax.broadcasted_iota(jnp.int32, (4 * LANES, LANES), 1)
    pick_head = (
        jnp.where(pick_row % LANES >= 64, groups, 0) + jnp.where(pick_row >= 2 * LANES, heads, 0)
    )

    def across(p, carry):
        @pl.when(pos == peers - 1)
        def _():
            hop_f(p).wait_recv()

        @pl.when(pos == 0)
        def _():
            hop_b(p).wait_recv()

        xs = join(*slabs(x_ref, p))
        dys = join(*slabs(dy_ref, p))
        gain_lo = gain_ref[:, pl.ds(pl.multiple_of(p * LANES, LANES), LANES)]
        gain_hi = gain_ref[:, pl.ds(pl.multiple_of(half + p * LANES, LANES), LANES)]
        gains = join(gain_lo, gain_hi)
        y_parts, dx_parts = [], []
        for j in range(2):
            g = 2 * p + j
            pick = (pick_col == pick_head + g).astype(BF16)
            start = state_in[g]
            carry_grad = prefix * grad_in[g]
            entered = (start, jnp.exp(total(g, 0)) * start + first_state[g])
            leaving = (later_grad[g] + jnp.exp(total(g, 1)) * carry_grad, carry_grad)
            y_rows, dx_rows = [], []
            for k in range(blocks):
                wi = by_head(wi_b, g, k)
                dt = by_head(dt_b, g, k)
                end = total(g, k)
                up = jnp.exp(wi)
                down = dt * jnp.exp(end - wi)
                e16 = entered[k].astype(BF16)
                g16 = leaving[k].astype(BF16)
                x = xs[j][span(k)]
                mask = mask_b[span(k), :]
                dy = dys[j][span(k)] * mask
                b_blk = b_ref[g, span(k), :]
                c_blk = c_ref[g, span(k), :]
                y = y_acc[g, span(k), :] + up * mm(c_blk, e16, 1, 0)
                dx_s = down * mm(b_blk, g16, 1, 0)
                dx = dx_acc[g, span(k), :] + dx_s
                dc_ref[g, span(k), :] += mm((dy * up).astype(BF16), e16, 1, 1)
                db_ref[g, span(k), :] += mm((x * down).astype(BF16), g16, 1, 1)
                q2 = x * dx
                extra = jnp.sum(x * dx_s, axis=0, keepdims=True) + jnp.exp(end) * jnp.sum(
                    leaving[k] * entered[k], axis=0, keepdims=True
                )
                q1 = dy * y - q2 + jnp.where(last, extra, 0.0)
                q1h = q1.astype(BF16)
                q2h = q2.astype(BF16)
                q1l = (q1 - q1h.astype(F32)).astype(BF16)
                q2l = (q2 - q2h.astype(F32)).astype(BF16)
                q_acc[span(k), :] += mm(jnp.concatenate([q1h, q1l, q2h, q2l], axis=1), pick, 1, 0)
                y_rows.append((y + gains[j] * x) * mask)
                dx_rows.append(dx + gains[j] * dy)
            y_parts.append(jnp.concatenate(y_rows, axis=0))
            dx_parts.append(jnp.concatenate(dx_rows, axis=0))
        for ref, parts in ((y_ref, y_parts), (dx_ref, dx_parts)):
            lo, hi = join(*parts)
            ref[:, pl.ds(pl.multiple_of(p * LANES, LANES), LANES)] = lo.astype(BF16)
            ref[:, pl.ds(pl.multiple_of(half + p * LANES, LANES), LANES)] = hi.astype(BF16)
        return carry

    lax.fori_loop(0, pairs, across, 0)

    for k in range(blocks):
        vals = small_ref[span(k), :]
        q = q_acc[span(k), :]
        d_log = lax.dot_general(
            tri.astype(F32), q, (((0,), (0,)), ((), ())),
            preferred_element_type=F32, precision=EXACT,
        )
        d_step = pltpu.roll(q, LANES - heads, 1)
        slope = pltpu.roll(vals, LANES - 2 * heads, 1)
        safe = jnp.where(vals > 0.0, vals, 1.0)
        gs_ref[span(k), :] = slope * (d_step / safe - decay_ref[...] * d_log)

    def finish(p, carry):
        @pl.when(pos < peers - 1)
        def _():
            hop_f(p).wait_send()

        @pl.when(pos > 0)
        def _():
            hop_b(p).wait_send()

        return carry

    lax.fori_loop(0, pairs, finish, 0)


def on_device(inputs, step_raw, decay_rate, skip_gain, b_proj, c_proj, lengths, cotangent):
    rows, width = inputs.shape
    heads = decay_rate.shape[0]
    groups, states = b_proj.shape[1:]
    peers = lax.axis_size("seq")
    position = lax.axis_index("seq")
    is_prefix = position < PREFIX_DEVS
    mine = lax.dynamic_slice_in_dim(lengths, jnp.maximum(position - PREFIX_DEVS, 0), 1)
    ids = jnp.arange(rows, dtype=jnp.int32)
    mask = jnp.where(jnp.logical_or(is_prefix, ids < mine[0]), 1.0, 0.0).astype(F32)[:, None]
    step = jax.nn.softplus(step_raw) * mask
    small = jnp.concatenate(
        [step, -(step * decay_rate[None, :]), jax.nn.sigmoid(step_raw) * mask,
         jnp.broadcast_to(mask, (rows, LANES - 3 * heads))], axis=1
    )
    gain = jnp.repeat(skip_gain, width // heads)[None, :]
    decay = jnp.pad(decay_rate, (0, LANES - heads))[None, :]
    b_lead = jnp.swapaxes(b_proj, 0, 1)
    c_lead = jnp.swapaxes(c_proj, 0, 1)
    vmem = pl.BlockSpec(memory_space=pltpu.VMEM)
    carry = pltpu.VMEM((groups, states, LANES), F32)
    dma = pltpu.SemaphoreType.DMA((groups // 2,))

    y, dx, gs, db, dc = pl.pallas_call(
        functools.partial(layer_kernel, peers, heads, groups),
        out_shape=(
            jax.ShapeDtypeStruct((rows, width), BF16),
            jax.ShapeDtypeStruct((rows, width), BF16),
            jax.ShapeDtypeStruct((rows, LANES), F32),
            jax.ShapeDtypeStruct((groups, rows, states), F32),
            jax.ShapeDtypeStruct((groups, rows, states), F32),
        ),
        in_specs=[vmem] * 7,
        out_specs=(vmem,) * 5,
        scratch_shapes=[
            pltpu.VMEM((heads, rows, LANES), F32),
            pltpu.VMEM((heads, rows, LANES), F32),
            pltpu.VMEM((LANES, rows), F32),
            pltpu.VMEM((LANES, rows), F32),
            carry, carry, carry, carry, carry, carry, carry, carry,
            pltpu.VMEM((groups, rows, LANES), F32),
            pltpu.VMEM((groups, rows, LANES), F32),
            pltpu.VMEM((rows, LANES), F32),
            pltpu.VMEM((rows, LANES), F32),
            dma, dma, dma, dma,
        ],
        compiler_params=pltpu.CompilerParams(
            collective_id=0, has_side_effects=True, vmem_limit_bytes=56 * 1024 * 1024
        ),
    )(inputs, cotangent, b_lead, c_lead, small, gain, decay)
    db = lax.psum_scatter(db, "head", scatter_dimension=1, tiled=True)
    dc = lax.psum_scatter(dc, "head", scatter_dimension=1, tiled=True)
    return (y, dx, gs[:, :heads], jnp.swapaxes(db, 0, 1), jnp.swapaxes(dc, 0, 1))


def solution(mesh):
    rows = P(("dp", "seq"), "head")
    proj = P(("dp", "seq"), None, None)
    grads = P(("dp", "seq", "head"), None, None)
    return jax.shard_map(
        on_device,
        mesh=mesh,
        in_specs=(rows, rows, P("head"), P("head"), proj, proj, P("dp"), rows),
        out_specs=(rows, rows, rows, grads, grads),
        check_vma=False,
    )
```

```python
import functools

import jax
import jax.numpy as jnp
from jax import lax
from jax.experimental import pallas as pl
from jax.experimental.pallas import tpu as pltpu
from jax.sharding import PartitionSpec as P

BLOCK = 256
PREFIX_DEVS = 2
LANES = 128
F32 = jnp.float32
BF16 = jnp.bfloat16
EXACT = lax.Precision.HIGHEST


def mm(a, b, ca, cb):
    return lax.dot_general(a, b, (((ca,), (cb,)), ((), ())), preferred_element_type=F32)


def layer_kernel(
    peers, ranks, heads, groups,
    x_ref, dy_ref, b_ref, c_ref, small_ref, gain_ref, decay_ref,
    y_ref, dx_ref, gs_ref, db_out, dc_out,
    wi_b, dt_b, wi_t, dt_t, state, first_state, grad_own, later_grad,
    state_in, state_out, grad_in, grad_out, y_acc, dx_acc, q_acc, mask_b,
    parts, arrived, fs_sem, fr_sem, bs_sem, br_sem, ps_sem, pr_sem,
):
    pos = lax.axis_index("seq")
    rank = lax.axis_index("head")
    prefix = jnp.where(pos < PREFIX_DEVS, 1.0, 0.0).astype(F32)
    rows = x_ref.shape[0]
    blocks = rows // BLOCK
    pairs = groups // 2
    half = groups * 64
    low = lax.broadcasted_iota(jnp.int32, (1, LANES), 1) < 64

    share = rows // ranks
    barrier = pltpu.get_barrier_semaphore()
    for away in range(1, ranks):
        pl.semaphore_signal(
            barrier, inc=1, device_id={"head": lax.rem(rank + away, ranks)},
            device_id_type=pl.DeviceIdType.MESH,
        )

    @pl.when(pos > 0)
    def _():
        pl.semaphore_signal(barrier, inc=1, device_id={"seq": pos - 1}, device_id_type=pl.DeviceIdType.MESH)

    @pl.when(pos < peers - 1)
    def _():
        pl.semaphore_signal(barrier, inc=1, device_id={"seq": pos + 1}, device_id_type=pl.DeviceIdType.MESH)

    tri = lax.broadcasted_iota(jnp.int32, (BLOCK, BLOCK), 0) >= lax.broadcasted_iota(
        jnp.int32, (BLOCK, BLOCK), 1
    )

    def span(k):
        return slice(k * BLOCK, (k + 1) * BLOCK)

    for k in range(blocks):
        vals = small_ref[span(k), :]
        sums = lax.dot_general(
            tri.astype(F32), vals, (((1,), (0,)), ((), ())),
            preferred_element_type=F32, precision=EXACT,
        )
        wi_t[:, span(k)] = sums.T
        dt_t[:, span(k)] = vals.T
        for h in range(heads):
            wi_b[h, span(k), :] = jnp.broadcast_to(sums[:, heads + h : heads + h + 1], (BLOCK, LANES))
            dt_b[h, span(k), :] = jnp.broadcast_to(vals[:, h : h + 1], (BLOCK, LANES))
        mask_b[span(k), :] = jnp.broadcast_to(vals[:, 3 * heads : 3 * heads + 1], (BLOCK, LANES))

    def turn(v):
        return pltpu.roll(v, 64, 1)

    def slabs(ref, p):
        lo = ref[:, pl.ds(pl.multiple_of(p * LANES, LANES), LANES)].astype(F32)
        hi = ref[:, pl.ds(pl.multiple_of(half + p * LANES, LANES), LANES)].astype(F32)
        return lo, hi

    def join(lo, hi):
        return jnp.where(low, lo, turn(hi)), jnp.where(low, turn(lo), hi)

    def by_head(ref, g, k):
        return jnp.where(low, ref[g, span(k), :], ref[groups + g, span(k), :])

    def total(g, k):
        at = pl.ds((k + 1) * BLOCK - 1, 1)
        return jnp.where(low, wi_b[g, at, :], wi_b[groups + g, at, :])

    def hop_f(p):
        part = pl.ds(2 * p, 2)
        return pltpu.make_async_remote_copy(
            src_ref=state_out.at[part], dst_ref=state_in.at[part],
            send_sem=fs_sem.at[p], recv_sem=fr_sem.at[p],
            device_id={"seq": pos + 1}, device_id_type=pl.DeviceIdType.MESH,
        )

    def hop_b(p):
        part = pl.ds(2 * p, 2)
        return pltpu.make_async_remote_copy(
            src_ref=grad_out.at[part], dst_ref=grad_in.at[part],
            send_sem=bs_sem.at[p], recv_sem=br_sem.at[p],
            device_id={"seq": pos - 1}, device_id_type=pl.DeviceIdType.MESH,
        )

    def give(g, away):
        to = lax.rem(rank + away, ranks)
        return pltpu.make_async_remote_copy(
            src_ref=parts.at[g, :, pl.ds(pl.multiple_of(to * share, share), share), :],
            dst_ref=arrived.at[away - 1, g],
            send_sem=ps_sem.at[away - 1, g], recv_sem=pr_sem.at[away - 1, g],
            device_id={"head": to}, device_id_type=pl.DeviceIdType.MESH,
        )

    def whole(g):
        return jnp.exp(prefix * (total(g, 0) + total(g, 1)))

    def pass_f(p):
        for j in range(2):
            g = 2 * p + j
            state_out[g] = whole(g) * state_in[g] + prefix * state[g]
        hop_f(p).start()

    def pass_b(p):
        for j in range(2):
            g = 2 * p + j
            grad_out[g] = whole(g) * grad_in[g] + grad_own[g]
        hop_b(p).start()

    @pl.when(pos == 0)
    def _():
        state_in[...] = jnp.zeros_like(state_in)

    @pl.when(pos == peers - 1)
    def _():
        grad_in[...] = jnp.zeros_like(grad_in)

    @pl.when(jnp.logical_or(pos == 0, pos == peers - 1))
    def _():
        pl.semaphore_wait(barrier, ranks)

    @pl.when(jnp.logical_and(pos > 0, pos < peers - 1))
    def _():
        pl.semaphore_wait(barrier, ranks + 1)

    def local_states(p, carry):
        xs = join(*slabs(x_ref, p))
        dys = join(*slabs(dy_ref, p))
        for j in range(2):
            g = 2 * p + j
            adds, backs = [], []
            for k in range(blocks):
                wi = by_head(wi_b, g, k)
                dt = by_head(dt_b, g, k)
                scaled = (xs[j][span(k)] * (dt * jnp.exp(total(g, k) - wi))).astype(BF16)
                adds.append(mm(b_ref[g, span(k), :], scaled, 0, 0))
                lifted = (dys[j][span(k)] * mask_b[span(k), :] * jnp.exp(wi)).astype(BF16)
                backs.append(mm(c_ref[g, span(k), :], lifted, 0, 0))
            first_state[g] = adds[0]
            state[g] = jnp.exp(total(g, 1)) * adds[0] + adds[1]
            later_grad[g] = backs[1]
            grad_own[g] = backs[0] + jnp.exp(total(g, 0)) * backs[1]

        @pl.when(pos == 0)
        def _():
            pass_f(p)

        @pl.when(pos == peers - 1)
        def _():
            pass_b(p)

        return carry

    lax.fori_loop(0, pairs, local_states, 0)

    def inside(p):
        xs = join(*slabs(x_ref, p))
        dys = join(*slabs(dy_ref, p))
        for j in range(2):
            g = 2 * p + j
            for k in range(blocks):
                b_blk = b_ref[g, span(k), :]
                c_blk = c_ref[g, span(k), :]
                scores = mm(c_blk, b_blk, 1, 1)
                x16 = xs[j][span(k)].astype(BF16)
                dyf = dys[j][span(k)] * mask_b[span(k), :]
                dy16 = dyf.astype(BF16)
                ys, dxs = [], []
                d_scores = None
                for m in range(2):
                    h = m * groups + g
                    col = wi_b[h, span(k), :]
                    col = jnp.concatenate([col, col], axis=1)
                    row = wi_t[pl.ds(heads + h, 1), span(k)]
                    decay = jnp.where(tri, jnp.exp(jnp.minimum(col - row, 0.0)), 0.0)
                    decay = decay * dt_t[pl.ds(h, 1), span(k)]
                    weights = (scores * decay).astype(BF16)
                    mine = low if m == 0 else jnp.logical_not(low)
                    dy_m = jnp.where(mine, dyf, 0.0).astype(BF16)
                    d_weights = mm(dy_m, x16, 1, 1) * decay
                    d_scores = d_weights if d_scores is None else d_scores + d_weights
                    ys.append(mm(weights, x16, 1, 0))
                    dxs.append(mm(weights, dy16, 0, 0))
                y_acc[g, span(k), :] = jnp.where(low, ys[0], ys[1])
                dx_acc[g, span(k), :] = jnp.where(low, dxs[0], dxs[1])
                ds16 = d_scores.astype(BF16)
                parts[g, 1, span(k), :] = mm(ds16, b_blk, 1, 0)
                parts[g, 0, span(k), :] = mm(ds16, c_blk, 0, 0)

    q_acc[...] = jnp.zeros_like(q_acc)
    last = lax.broadcasted_iota(jnp.int32, (BLOCK, 1), 0) == BLOCK - 1
    pick_row = lax.broadcasted_iota(jnp.int32, (4 * LANES, LANES), 0)
    pick_col = lax.broadcasted_iota(jnp.int32, (4 * LANES, LANES), 1)
    pick_head = (
        jnp.where(pick_row % LANES >= 64, groups, 0) + jnp.where(pick_row >= 2 * LANES, heads, 0)
    )

    def across(p):
        @pl.when(pos == peers - 1)
        def _():
            hop_f(p).wait_recv()

        @pl.when(pos == 0)
        def _():
            hop_b(p).wait_recv()

        xs = join(*slabs(x_ref, p))
        dys = join(*slabs(dy_ref, p))
        gain_lo = gain_ref[:, pl.ds(pl.multiple_of(p * LANES, LANES), LANES)]
        gain_hi = gain_ref[:, pl.ds(pl.multiple_of(half + p * LANES, LANES), LANES)]
        gains = join(gain_lo, gain_hi)
        y_parts, dx_parts = [], []
        for j in range(2):
            g = 2 * p + j
            pick = (pick_col == pick_head + g).astype(BF16)
            start = state_in[g]
            carry_grad = prefix * grad_in[g]
            entered = (start, jnp.exp(total(g, 0)) * start + first_state[g])
            leaving = (later_grad[g] + jnp.exp(total(g, 1)) * carry_grad, carry_grad)
            y_rows, dx_rows = [], []
            for k in range(blocks):
                wi = by_head(wi_b, g, k)
                dt = by_head(dt_b, g, k)
                end = total(g, k)
                up = jnp.exp(wi)
                down = dt * jnp.exp(end - wi)
                e16 = entered[k].astype(BF16)
                g16 = leaving[k].astype(BF16)
                x = xs[j][span(k)]
                mask = mask_b[span(k), :]
                dy = dys[j][span(k)] * mask
                b_blk = b_ref[g, span(k), :]
                c_blk = c_ref[g, span(k), :]
                y = y_acc[g, span(k), :] + up * mm(c_blk, e16, 1, 0)
                dx_s = down * mm(b_blk, g16, 1, 0)
                dx = dx_acc[g, span(k), :] + dx_s
                parts[g, 1, span(k), :] += mm((dy * up).astype(BF16), e16, 1, 1)
                parts[g, 0, span(k), :] += mm((x * down).astype(BF16), g16, 1, 1)
                q2 = x * dx
                extra = jnp.sum(x * dx_s, axis=0, keepdims=True) + jnp.exp(end) * jnp.sum(
                    leaving[k] * entered[k], axis=0, keepdims=True
                )
                q1 = dy * y - q2 + jnp.where(last, extra, 0.0)
                q1h = q1.astype(BF16)
                q2h = q2.astype(BF16)
                q1l = (q1 - q1h.astype(F32)).astype(BF16)
                q2l = (q2 - q2h.astype(F32)).astype(BF16)
                q_acc[span(k), :] += mm(jnp.concatenate([q1h, q1l, q2h, q2l], axis=1), pick, 1, 0)
                y_rows.append((y + gains[j] * x) * mask)
                dx_rows.append(dx + gains[j] * dy)
            for away in range(1, ranks):
                give(g, away).start()
            y_parts.append(jnp.concatenate(y_rows, axis=0))
            dx_parts.append(jnp.concatenate(dx_rows, axis=0))
        for ref, pair in ((y_ref, y_parts), (dx_ref, dx_parts)):
            lo, hi = join(*pair)
            ref[:, pl.ds(pl.multiple_of(p * LANES, LANES), LANES)] = lo.astype(BF16)
            ref[:, pl.ds(pl.multiple_of(half + p * LANES, LANES), LANES)] = hi.astype(BF16)

    lag = max(1, peers - 3)
    middle = jnp.logical_and(pos > 0, pos < peers - 1)

    def stage(s, carry):
        pf = s - (pos - 1)
        pb = s - (peers - 2 - pos)

        @pl.when(jnp.logical_and(middle, jnp.logical_and(pf >= 0, pf < pairs)))
        def _():
            hop_f(pf).wait_recv()
            pass_f(pf)

        @pl.when(jnp.logical_and(middle, jnp.logical_and(pb >= 0, pb < pairs)))
        def _():
            hop_b(pb).wait_recv()
            pass_b(pb)

        @pl.when(s < pairs)
        def _():
            inside(s)

        @pl.when(jnp.logical_and(s >= lag, s < pairs + lag))
        def _():
            across(s - lag)

        return carry

    lax.fori_loop(0, pairs + lag, stage, 0)

    for k in range(blocks):
        vals = small_ref[span(k), :]
        q = q_acc[span(k), :]
        d_log = lax.dot_general(
            tri.astype(F32), q, (((0,), (0,)), ((), ())),
            preferred_element_type=F32, precision=EXACT,
        )
        d_step = pltpu.roll(q, LANES - heads, 1)
        slope = pltpu.roll(vals, LANES - 2 * heads, 1)
        safe = jnp.where(vals > 0.0, vals, 1.0)
        gs_ref[span(k), :] = slope * (d_step / safe - decay_ref[...] * d_log)

    own = pl.ds(pl.multiple_of(rank * share, share), share)
    for g in range(groups):
        db = parts[g, 0, own, :]
        dc = parts[g, 1, own, :]
        for away in range(1, ranks):
            give(g, away).wait_recv()
            db = db + arrived[away - 1, g, 0]
            dc = dc + arrived[away - 1, g, 1]
        db_out[:, g, :] = db
        dc_out[:, g, :] = dc
    for g in range(groups):
        for away in range(1, ranks):
            give(g, away).wait_send()

    def finish(p, carry):
        @pl.when(pos < peers - 1)
        def _():
            hop_f(p).wait_send()

        @pl.when(pos > 0)
        def _():
            hop_b(p).wait_send()

        return carry

    lax.fori_loop(0, pairs, finish, 0)


def on_device(inputs, step_raw, decay_rate, skip_gain, b_proj, c_proj, lengths, cotangent):
    rows, width = inputs.shape
    heads = decay_rate.shape[0]
    groups, states = b_proj.shape[1:]
    peers = lax.axis_size("seq")
    ranks = lax.axis_size("head")
    position = lax.axis_index("seq")
    is_prefix = position < PREFIX_DEVS
    mine = lax.dynamic_slice_in_dim(lengths, jnp.maximum(position - PREFIX_DEVS, 0), 1)
    ids = jnp.arange(rows, dtype=jnp.int32)
    mask = jnp.where(jnp.logical_or(is_prefix, ids < mine[0]), 1.0, 0.0).astype(F32)[:, None]
    step = jax.nn.softplus(step_raw) * mask
    small = jnp.concatenate(
        [step, -(step * decay_rate[None, :]), jax.nn.sigmoid(step_raw) * mask,
         jnp.broadcast_to(mask, (rows, LANES - 3 * heads))], axis=1
    )
    gain = jnp.repeat(skip_gain, width // heads)[None, :]
    decay = jnp.pad(decay_rate, (0, LANES - heads))[None, :]
    b_lead = jnp.swapaxes(b_proj, 0, 1)
    c_lead = jnp.swapaxes(c_proj, 0, 1)
    vmem = pl.BlockSpec(memory_space=pltpu.VMEM)
    carry = pltpu.VMEM((groups, states, LANES), F32)
    dma = pltpu.SemaphoreType.DMA((groups // 2,))

    y, dx, gs, db, dc = pl.pallas_call(
        functools.partial(layer_kernel, peers, ranks, heads, groups),
        out_shape=(
            jax.ShapeDtypeStruct((rows, width), BF16),
            jax.ShapeDtypeStruct((rows, width), BF16),
            jax.ShapeDtypeStruct((rows, LANES), F32),
            jax.ShapeDtypeStruct((rows // ranks, groups, states), F32),
            jax.ShapeDtypeStruct((rows // ranks, groups, states), F32),
        ),
        in_specs=[vmem] * 7,
        out_specs=(vmem,) * 5,
        scratch_shapes=[
            pltpu.VMEM((heads, rows, LANES), F32),
            pltpu.VMEM((heads, rows, LANES), F32),
            pltpu.VMEM((LANES, rows), F32),
            pltpu.VMEM((LANES, rows), F32),
            carry, carry, carry, carry, carry, carry, carry, carry,
            pltpu.VMEM((groups, rows, LANES), F32),
            pltpu.VMEM((groups, rows, LANES), F32),
            pltpu.VMEM((rows, LANES), F32),
            pltpu.VMEM((rows, LANES), F32),
            pltpu.VMEM((groups, 2, rows, states), F32),
            pltpu.VMEM((ranks - 1, groups, 2, rows // ranks, states), F32),
            dma, dma, dma, dma,
            pltpu.SemaphoreType.DMA((ranks - 1, groups)),
            pltpu.SemaphoreType.DMA((ranks - 1, groups)),
        ],
        compiler_params=pltpu.CompilerParams(
            collective_id=0, has_side_effects=True, vmem_limit_bytes=56 * 1024 * 1024
        ),
    )(inputs, cotangent, b_lead, c_lead, small, gain, decay)
    return (y, dx, gs[:, :heads], db, dc)


def solution(mesh):
    rows = P(("dp", "seq"), "head")
    proj = P(("dp", "seq"), None, None)
    grads = P(("dp", "seq", "head"), None, None)
    return jax.shard_map(
        on_device,
        mesh=mesh,
        in_specs=(rows, rows, P("head"), P("head"), proj, proj, P("dp"), rows),
        out_specs=(rows, rows, rows, grads, grads),
        check_vma=False,
    )
```

```python
import functools

import jax
import jax.numpy as jnp
from jax import lax
from jax.experimental import pallas as pl
from jax.experimental.pallas import tpu as pltpu
from jax.sharding import PartitionSpec as P

BLOCK = 256
PREFIX_DEVS = 2
LANES = 128
F32 = jnp.float32
BF16 = jnp.bfloat16
EXACT = lax.Precision.HIGHEST


def mm(a, b, ca, cb):
    return lax.dot_general(a, b, (((ca,), (cb,)), ((), ())), preferred_element_type=F32)


def layer_kernel(
    peers, ranks, heads, groups,
    x_ref, dy_ref, b_ref, c_ref, step_ref, gain_ref, decay_ref, lengths_ref,
    y_ref, dx_ref, gs_ref, db_out, dc_out,
    wi_b, dt_b, wi_t, dt_t, state, first_state, grad_own, later_grad,
    state_in, state_out, grad_in, grad_out, y_acc, dx_acc, q_acc, mask_b, gain_b, decay_b,
    parts, arrived, summed, fs_sem, fr_sem, bs_sem, br_sem, ps_sem, pr_sem, ss_sem, sr_sem,
):
    pos = lax.axis_index("seq")
    rank = lax.axis_index("head")
    prefix = jnp.where(pos < PREFIX_DEVS, 1.0, 0.0).astype(F32)
    rows = x_ref.shape[0]
    blocks = rows // BLOCK
    pairs = groups // 2
    half = groups * 64
    low = lax.broadcasted_iota(jnp.int32, (1, LANES), 1) < 64

    share = rows // ranks
    barrier = pltpu.get_barrier_semaphore()
    for away in range(1, ranks):
        pl.semaphore_signal(
            barrier, inc=1, device_id={"head": lax.rem(rank + away, ranks)},
            device_id_type=pl.DeviceIdType.MESH,
        )

    @pl.when(pos > 0)
    def _():
        pl.semaphore_signal(barrier, inc=1, device_id={"seq": pos - 1}, device_id_type=pl.DeviceIdType.MESH)

    @pl.when(pos < peers - 1)
    def _():
        pl.semaphore_signal(barrier, inc=1, device_id={"seq": pos + 1}, device_id_type=pl.DeviceIdType.MESH)

    tri = lax.broadcasted_iota(jnp.int32, (BLOCK, BLOCK), 0) >= lax.broadcasted_iota(
        jnp.int32, (BLOCK, BLOCK), 1
    )

    def span(k):
        return slice(k * BLOCK, (k + 1) * BLOCK)

    limit = jnp.where(pos < PREFIX_DEVS, rows, lengths_ref[jnp.maximum(pos - PREFIX_DEVS, 0)])
    ids = lax.broadcasted_iota(jnp.int32, (1, BLOCK), 1)
    for h in range(heads):
        gain_b[h : h + 1, :] = jnp.full((1, LANES), gain_ref[h], F32)
        decay_b[h : h + 1, :] = jnp.full((1, LANES), decay_ref[h], F32)
    rate = jnp.concatenate([decay_b[...]] * (BLOCK // LANES), axis=1)

    def kept(k):
        return jnp.where(ids + k * BLOCK < limit, 1.0, 0.0).astype(F32)

    for k in range(blocks):
        raw = step_ref[:, span(k)]
        keep = kept(k)
        step = (jnp.maximum(raw, 0.0) + jnp.log1p(jnp.exp(-jnp.abs(raw)))) * keep
        sums = lax.dot_general(
            -(step * rate), tri.astype(F32), (((1,), (1,)), ((), ())),
            preferred_element_type=F32, precision=EXACT,
        )
        wi_t[:, span(k)] = sums
        dt_t[:, span(k)] = step
        tall = jnp.concatenate(
            [step, sums, jnp.broadcast_to(keep, (LANES - 2 * heads, BLOCK))], axis=0
        ).T
        for h in range(heads):
            wi_b[h, span(k), :] = jnp.broadcast_to(tall[:, heads + h : heads + h + 1], (BLOCK, LANES))
            dt_b[h, span(k), :] = jnp.broadcast_to(tall[:, h : h + 1], (BLOCK, LANES))
        mask_b[span(k), :] = jnp.broadcast_to(tall[:, 2 * heads : 2 * heads + 1], (BLOCK, LANES))

    def turn(v):
        return pltpu.roll(v, 64, 1)

    def slabs(ref, p):
        lo = ref[:, pl.ds(pl.multiple_of(p * LANES, LANES), LANES)].astype(F32)
        hi = ref[:, pl.ds(pl.multiple_of(half + p * LANES, LANES), LANES)].astype(F32)
        return lo, hi

    def join(lo, hi):
        return jnp.where(low, lo, turn(hi)), jnp.where(low, turn(lo), hi)

    def by_head(ref, g, k):
        return jnp.where(low, ref[g, span(k), :], ref[groups + g, span(k), :])

    def total(g, k):
        at = pl.ds((k + 1) * BLOCK - 1, 1)
        return jnp.where(low, wi_b[g, at, :], wi_b[groups + g, at, :])

    def hop_f(p):
        part = pl.ds(2 * p, 2)
        return pltpu.make_async_remote_copy(
            src_ref=state_out.at[part], dst_ref=state_in.at[part],
            send_sem=fs_sem.at[p], recv_sem=fr_sem.at[p],
            device_id={"seq": pos + 1}, device_id_type=pl.DeviceIdType.MESH,
        )

    def hop_b(p):
        part = pl.ds(2 * p, 2)
        return pltpu.make_async_remote_copy(
            src_ref=grad_out.at[part], dst_ref=grad_in.at[part],
            send_sem=bs_sem.at[p], recv_sem=br_sem.at[p],
            device_id={"seq": pos - 1}, device_id_type=pl.DeviceIdType.MESH,
        )

    def give(g, away):
        to = lax.rem(rank + away, ranks)
        return pltpu.make_async_remote_copy(
            src_ref=parts.at[g, :, pl.ds(pl.multiple_of(to * share, share), share), :],
            dst_ref=arrived.at[away - 1, g],
            send_sem=ps_sem.at[away - 1, g], recv_sem=pr_sem.at[away - 1, g],
            device_id={"head": to}, device_id_type=pl.DeviceIdType.MESH,
        )

    def piece(g, kind, owner):
        return parts.at[g, kind, pl.ds(pl.multiple_of(owner * share, share), share), :]

    def flip(bit):
        low_bit = lax.rem(rank, 2)
        if bit == 1:
            return rank + 1 - 2 * low_bit
        if bit == 2:
            return lax.rem(rank + 2, 4)
        return lax.rem(rank + 2, 4) + 1 - 2 * low_bit

    def first_hop(g, kind, which):
        to = flip(kind + 1)
        return pltpu.make_async_remote_copy(
            src_ref=piece(g, kind, to if which == 0 else flip(3)),
            dst_ref=arrived.at[which, g, kind],
            send_sem=ps_sem.at[2 * kind + which, g], recv_sem=pr_sem.at[2 * kind + which, g],
            device_id={"head": to}, device_id_type=pl.DeviceIdType.MESH,
        )

    def second_hop(g, kind):
        to = flip(2 - kind)
        return pltpu.make_async_remote_copy(
            src_ref=piece(g, kind, to), dst_ref=summed.at[g, kind],
            send_sem=ss_sem.at[kind, g], recv_sem=sr_sem.at[kind, g],
            device_id={"head": to}, device_id_type=pl.DeviceIdType.MESH,
        )

    square = ranks == 4

    def send_group(g):
        if square:
            for which in (1, 0):
                for kind in range(2):
                    first_hop(g, kind, which).start()
        else:
            for away in range(1, ranks):
                give(g, away).start()

    def forward_group(g):
        if square:
            for kind in range(2):
                first_hop(g, kind, 1).wait_recv()
                at = pl.ds(pl.multiple_of(flip(2 - kind) * share, share), share)
                parts[g, kind, at, :] += arrived[1, g, kind]
                second_hop(g, kind).start()

    def collect_group(g):
        own = pl.ds(pl.multiple_of(rank * share, share), share)
        for kind, out in enumerate((db_out, dc_out)):
            val = parts[g, kind, own, :]
            if square:
                first_hop(g, kind, 0).wait_recv()
                second_hop(g, kind).wait_recv()
                val = val + arrived[0, g, kind] + summed[g, kind]
            else:
                if kind == 0:
                    for away in range(1, ranks):
                        give(g, away).wait_recv()
                for away in range(1, ranks):
                    val = val + arrived[away - 1, g, kind]
            out[:, g, :] = val

    def settle_group(g):
        if square:
            for kind in range(2):
                for which in range(2):
                    first_hop(g, kind, which).wait_send()
                second_hop(g, kind).wait_send()
        else:
            for away in range(1, ranks):
                give(g, away).wait_send()

    def whole(g):
        return jnp.exp(prefix * (total(g, 0) + total(g, 1)))

    def pass_f(p):
        for j in range(2):
            g = 2 * p + j
            state_out[g] = whole(g) * state_in[g] + prefix * state[g]
        hop_f(p).start()

    def pass_b(p):
        for j in range(2):
            g = 2 * p + j
            grad_out[g] = whole(g) * grad_in[g] + grad_own[g]
        hop_b(p).start()

    @pl.when(pos == 0)
    def _():
        state_in[...] = jnp.zeros_like(state_in)

    @pl.when(pos == peers - 1)
    def _():
        grad_in[...] = jnp.zeros_like(grad_in)

    @pl.when(jnp.logical_or(pos == 0, pos == peers - 1))
    def _():
        pl.semaphore_wait(barrier, ranks)

    @pl.when(jnp.logical_and(pos > 0, pos < peers - 1))
    def _():
        pl.semaphore_wait(barrier, ranks + 1)

    def local_states(p, carry):
        xs = join(*slabs(x_ref, p))
        dys = join(*slabs(dy_ref, p))
        for j in range(2):
            g = 2 * p + j
            adds, backs = [], []
            for k in range(blocks):
                wi = by_head(wi_b, g, k)
                dt = by_head(dt_b, g, k)
                scaled = (xs[j][span(k)] * (dt * jnp.exp(total(g, k) - wi))).astype(BF16)
                adds.append(mm(b_ref[g, span(k), :], scaled, 0, 0))
                lifted = (dys[j][span(k)] * mask_b[span(k), :] * jnp.exp(wi)).astype(BF16)
                backs.append(mm(c_ref[g, span(k), :], lifted, 0, 0))
            first_state[g] = adds[0]
            state[g] = jnp.exp(total(g, 1)) * adds[0] + adds[1]
            later_grad[g] = backs[1]
            grad_own[g] = backs[0] + jnp.exp(total(g, 0)) * backs[1]

        @pl.when(pos == 0)
        def _():
            pass_f(p)

        @pl.when(pos == peers - 1)
        def _():
            pass_b(p)

        return carry

    lax.fori_loop(0, pairs, local_states, 0)

    def inside(p):
        xs = join(*slabs(x_ref, p))
        dys = join(*slabs(dy_ref, p))
        for j in range(2):
            g = 2 * p + j
            for k in range(blocks):
                b_blk = b_ref[g, span(k), :]
                c_blk = c_ref[g, span(k), :]
                scores = mm(c_blk, b_blk, 1, 1)
                x16 = xs[j][span(k)].astype(BF16)
                dyf = dys[j][span(k)] * mask_b[span(k), :]
                dy16 = dyf.astype(BF16)
                ys, dxs = [], []
                d_scores = None
                for m in range(2):
                    h = m * groups + g
                    col = wi_b[h, span(k), :]
                    col = jnp.concatenate([col, col], axis=1)
                    row = wi_t[pl.ds(h, 1), span(k)]
                    decay = jnp.where(tri, jnp.exp(jnp.minimum(col - row, 0.0)), 0.0)
                    decay = decay * dt_t[pl.ds(h, 1), span(k)]
                    weights = (scores * decay).astype(BF16)
                    mine = low if m == 0 else jnp.logical_not(low)
                    dy_m = jnp.where(mine, dyf, 0.0).astype(BF16)
                    d_weights = mm(dy_m, x16, 1, 1) * decay
                    d_scores = d_weights if d_scores is None else d_scores + d_weights
                    ys.append(mm(weights, x16, 1, 0))
                    dxs.append(mm(weights, dy16, 0, 0))
                y_acc[g, span(k), :] = jnp.where(low, ys[0], ys[1])
                dx_acc[g, span(k), :] = jnp.where(low, dxs[0], dxs[1])
                ds16 = d_scores.astype(BF16)
                parts[g, 1, span(k), :] = mm(ds16, b_blk, 1, 0)
                parts[g, 0, span(k), :] = mm(ds16, c_blk, 0, 0)

    q_acc[...] = jnp.zeros_like(q_acc)
    last = lax.broadcasted_iota(jnp.int32, (BLOCK, 1), 0) == BLOCK - 1
    pick_row = lax.broadcasted_iota(jnp.int32, (4 * LANES, LANES), 0)
    pick_col = lax.broadcasted_iota(jnp.int32, (4 * LANES, LANES), 1)
    pick_head = (
        jnp.where(pick_row % LANES >= 64, groups, 0) + jnp.where(pick_row >= 2 * LANES, heads, 0)
    )

    def across(p):
        @pl.when(pos == peers - 1)
        def _():
            hop_f(p).wait_recv()

        @pl.when(pos == 0)
        def _():
            hop_b(p).wait_recv()

        xs = join(*slabs(x_ref, p))
        dys = join(*slabs(dy_ref, p))
        y_parts, dx_parts = [], []
        for j in range(2):
            g = 2 * p + j
            pick = (pick_col == pick_head + g).astype(BF16)
            gain = jnp.where(low, gain_b[pl.ds(g, 1), :], gain_b[pl.ds(groups + g, 1), :])
            start = state_in[g]
            carry_grad = prefix * grad_in[g]
            entered = (start, jnp.exp(total(g, 0)) * start + first_state[g])
            leaving = (later_grad[g] + jnp.exp(total(g, 1)) * carry_grad, carry_grad)
            y_rows, dx_rows = [], []
            for k in range(blocks):
                wi = by_head(wi_b, g, k)
                dt = by_head(dt_b, g, k)
                end = total(g, k)
                up = jnp.exp(wi)
                down = dt * jnp.exp(end - wi)
                e16 = entered[k].astype(BF16)
                g16 = leaving[k].astype(BF16)
                x = xs[j][span(k)]
                mask = mask_b[span(k), :]
                dy = dys[j][span(k)] * mask
                b_blk = b_ref[g, span(k), :]
                c_blk = c_ref[g, span(k), :]
                y = y_acc[g, span(k), :] + up * mm(c_blk, e16, 1, 0)
                dx_s = down * mm(b_blk, g16, 1, 0)
                dx = dx_acc[g, span(k), :] + dx_s
                parts[g, 1, span(k), :] += mm((dy * up).astype(BF16), e16, 1, 1)
                parts[g, 0, span(k), :] += mm((x * down).astype(BF16), g16, 1, 1)
                q2 = x * dx
                extra = jnp.sum(x * dx_s, axis=0, keepdims=True) + jnp.exp(end) * jnp.sum(
                    leaving[k] * entered[k], axis=0, keepdims=True
                )
                q1 = dy * y - q2 + jnp.where(last, extra, 0.0)
                q1h = q1.astype(BF16)
                q2h = q2.astype(BF16)
                q1l = (q1 - q1h.astype(F32)).astype(BF16)
                q2l = (q2 - q2h.astype(F32)).astype(BF16)
                q_acc[span(k), :] += mm(jnp.concatenate([q1h, q1l, q2h, q2l], axis=1), pick, 1, 0)
                y_rows.append((y + gain * x) * mask)
                dx_rows.append(dx + gain * dy)
            send_group(g)
            y_parts.append(jnp.concatenate(y_rows, axis=0))
            dx_parts.append(jnp.concatenate(dx_rows, axis=0))
        for ref, pair in ((y_ref, y_parts), (dx_ref, dx_parts)):
            lo, hi = join(*pair)
            ref[:, pl.ds(pl.multiple_of(p * LANES, LANES), LANES)] = lo.astype(BF16)
            ref[:, pl.ds(pl.multiple_of(half + p * LANES, LANES), LANES)] = hi.astype(BF16)

    lag = max(1, peers - 3)
    middle = jnp.logical_and(pos > 0, pos < peers - 1)

    def stage(s, carry):
        pf = s - (pos - 1)
        pb = s - (peers - 2 - pos)

        @pl.when(jnp.logical_and(middle, jnp.logical_and(pf >= 0, pf < pairs)))
        def _():
            hop_f(pf).wait_recv()
            pass_f(pf)

        @pl.when(jnp.logical_and(middle, jnp.logical_and(pb >= 0, pb < pairs)))
        def _():
            hop_b(pb).wait_recv()
            pass_b(pb)

        @pl.when(s < pairs)
        def _():
            inside(s)

        @pl.when(jnp.logical_and(s >= lag, s < pairs + lag))
        def _():
            across(s - lag)

        @pl.when(jnp.logical_and(s > lag, s < pairs + lag))
        def _():
            for j in range(2):
                forward_group(2 * (s - lag - 1) + j)

        return carry

    lax.fori_loop(0, pairs + lag, stage, 0)
    for g in range(groups - 2, groups):
        forward_group(g)

    for k in range(blocks):
        q = q_acc[span(k), :].T
        step = dt_t[:, span(k)]
        d_log = lax.dot_general(
            q[:heads], tri.astype(F32), (((1,), (0,)), ((), ())),
            preferred_element_type=F32, precision=EXACT,
        )
        slope = jax.nn.sigmoid(step_ref[:, span(k)]) * kept(k)
        safe = jnp.where(step > 0.0, step, 1.0)
        gs_ref[:, span(k)] = slope * (q[heads : 2 * heads] / safe - rate * d_log)

    for g in range(groups):
        collect_group(g)
    for g in range(groups):
        settle_group(g)

    def finish(p, carry):
        @pl.when(pos < peers - 1)
        def _():
            hop_f(p).wait_send()

        @pl.when(pos > 0)
        def _():
            hop_b(p).wait_send()

        return carry

    lax.fori_loop(0, pairs, finish, 0)


def on_device(inputs, step_raw, decay_rate, skip_gain, b_proj, c_proj, lengths, cotangent):
    rows, width = inputs.shape
    heads = decay_rate.shape[0]
    groups, states = b_proj.shape[1:]
    peers = lax.axis_size("seq")
    ranks = lax.axis_size("head")
    hops = 2 if ranks == 4 else ranks - 1
    b_lead = jnp.swapaxes(b_proj, 0, 1)
    c_lead = jnp.swapaxes(c_proj, 0, 1)
    vmem = pl.BlockSpec(memory_space=pltpu.VMEM)
    smem = pl.BlockSpec(memory_space=pltpu.SMEM)
    carry = pltpu.VMEM((groups, states, LANES), F32)
    dma = pltpu.SemaphoreType.DMA((groups // 2,))

    y, dx, gs, db, dc = pl.pallas_call(
        functools.partial(layer_kernel, peers, ranks, heads, groups),
        out_shape=(
            jax.ShapeDtypeStruct((rows, width), BF16),
            jax.ShapeDtypeStruct((rows, width), BF16),
            jax.ShapeDtypeStruct((heads, rows), F32),
            jax.ShapeDtypeStruct((rows // ranks, groups, states), F32),
            jax.ShapeDtypeStruct((rows // ranks, groups, states), F32),
        ),
        in_specs=[vmem] * 5 + [smem] * 3,
        out_specs=(vmem,) * 5,
        scratch_shapes=[
            pltpu.VMEM((heads, rows, LANES), F32),
            pltpu.VMEM((heads, rows, LANES), F32),
            pltpu.VMEM((heads, rows), F32),
            pltpu.VMEM((heads, rows), F32),
            carry, carry, carry, carry, carry, carry, carry, carry,
            pltpu.VMEM((groups, rows, LANES), F32),
            pltpu.VMEM((groups, rows, LANES), F32),
            pltpu.VMEM((rows, LANES), F32),
            pltpu.VMEM((rows, LANES), F32),
            pltpu.VMEM((heads, LANES), F32),
            pltpu.VMEM((heads, LANES), F32),
            pltpu.VMEM((groups, 2, rows, states), F32),
            pltpu.VMEM((hops, groups, 2, rows // ranks, states), F32),
            pltpu.VMEM((groups, 2, rows // ranks, states), F32),
            dma, dma, dma, dma,
            pltpu.SemaphoreType.DMA((max(ranks - 1, 4), groups)),
            pltpu.SemaphoreType.DMA((max(ranks - 1, 4), groups)),
            pltpu.SemaphoreType.DMA((2, groups)),
            pltpu.SemaphoreType.DMA((2, groups)),
        ],
        compiler_params=pltpu.CompilerParams(
            collective_id=0, has_side_effects=True, vmem_limit_bytes=56 * 1024 * 1024
        ),
    )(
        inputs, cotangent, b_lead, c_lead, step_raw.T, skip_gain, decay_rate, lengths
    )
    return (y, dx, gs.T, db, dc)


def solution(mesh):
    rows = P(("dp", "seq"), "head")
    proj = P(("dp", "seq"), None, None)
    grads = P(("dp", "seq", "head"), None, None)
    return jax.shard_map(
        on_device,
        mesh=mesh,
        in_specs=(rows, rows, P("head"), P("head"), proj, proj, P("dp"), rows),
        out_specs=(rows, rows, rows, grads, grads),
        check_vma=False,
    )
```
